32 devices in a mesh: gx: 8 (over z, x), af: 4 (over y, core).
Axes of the slice: x: 2, y: 2, z: 4, core: 2. Of those that a mesh axis runs over, the one named last changes fastest.
Arguments:
- forcing: float32 [16, 2, 32, 5, 4, 256], P('af', None, 'gx'), may hold values from -6 to 6
- flow: float32 [32, 4, 256], P('gx'), may hold values from 0.2 to 1
- sponge: float32 [32, 4, 256], P('gx'), may hold values from 0.05 to 0.5
- coupling: float32 [5, 5], replicated, may hold values from -1.5 to 1.5
- omega: float32 [2], replicated, may hold values from 1 to 1.6
Outputs:
- basis: float32 [16, 2, 32, 5, 4, 256], P('af', None, 'gx')
- coeff: float32 [16, 16], replicated
The draws below stay inside these ranges and needn't reach their ends.
All inputs are finite; a program needn't handle non-finite values.
Results may differ from the reference program's by a relative error of at most 0.0001.
Values sent between devices are 32-bit elements; how exact they have to be, the bound alone decides.
No kernel may reach another device: no remote copies, remote signals or barrier semaphores. Data moves between devices by JAX's collectives and lax.ppermute only.
A program may use at most 64 MiB of HBM per device.

```python
import math
import jax
import jax.numpy as jnp
from jax import lax

V = 5
FORCINGS = 8
FREQS = 2
SWEEPS = 8
R = 4
TH = 256
COLS = 16
NX = 32


def levels(own_key, extent, pieces, low, high):
    factor_of, own = 1.0, jax.random.fold_in(own_key, 6)
    for dim, parts in pieces:
        steps = jnp.exp(jax.random.uniform(jax.random.fold_in(own, dim), (parts,), jnp.float32, low / len(pieces), high / len(pieces)))
        factor_of = factor_of * jnp.repeat(steps, extent[dim] // parts).reshape([-1 if axis == dim else 1 for axis in range(len(extent))])
    return factor_of


def normal_values(rng, dims, deviation, most, cuts=(), held_as=jnp.bfloat16):
    entries = jax.random.normal(rng, dims, jnp.float32) * deviation
    if len(cuts) > 0:
        entries = levels(rng, dims, cuts, -0.22, 0.18) * entries
    return jnp.clip(entries, min=-most, max=most).astype(held_as)


def setup_inputs(seed: int = 0) -> dict:
    splits = jax.random.split(jax.random.key(seed), 6)
    forcing = normal_values(splits[0], (COLS, 2, NX, V, R, TH), 1.0, 6.0, ((0, 4), (2, 8)), jnp.float32)
    flow = jnp.clip(0.2 + 0.8 * jax.random.uniform(splits[1], (NX, R, TH), jnp.float32) ** levels(splits[1], (NX, R, TH), ((0, 8),), -0.2, 0.2), 0.2, 1.0)
    sponge = jnp.clip(jnp.exp(math.log(0.5) - 2.3025851 * jax.random.uniform(splits[2], (NX, R, TH), jnp.float32) ** levels(splits[2], (NX, R, TH), ((0, 8),), -0.2, 0.2)), 0.05, 0.5)
    coupling = normal_values(splits[3], (V, V), 0.1, 1.5, (), jnp.float32)
    omega = jnp.clip(jax.random.uniform(splits[4], (FREQS,), jnp.float32, 1.0, 1.6), 1.0, 1.6)
    return dict(forcing=forcing, flow=flow, sponge=sponge, coupling=coupling, omega=omega)


viscosity = 0.25

def apply_adjoint(padded, freq, flow, sponge, coupling):
    field = padded[:, 1:-1]
    upper = padded[:, 2:]
    lower = padded[:, :-2]
    radial = jnp.pad(field, ((0, 0), (0, 0), (0, 0), (1, 1), (0, 0)))
    lap = upper + lower + radial[:, :, :, 2:, :] + radial[:, :, :, :-2, :]
    lap = lap + jnp.roll(field, 1, -1) + jnp.roll(field, -1, -1) - 6.0 * field
    advect = 0.5 * flow[:, None] * (lower - upper)
    mixed = jnp.einsum('wv,pxwrt->pxvrt', coupling, field, precision=lax.Precision.HIGHEST)
    rotate = jnp.stack([freq * field[1], -freq * field[0]])
    return sponge[:, None] * field + rotate - mixed + advect - viscosity * lap

def precondition(resid, freq, sponge, coupling):
    diag_re = sponge[:, None] + 6.0 * viscosity - jnp.diagonal(coupling)[None, :, None, None]
    denom = diag_re * diag_re + freq * freq
    p_re = diag_re / denom
    p_im = freq / denom
    return jnp.stack([p_re * resid[0] - p_im * resid[1], p_re * resid[1] + p_im * resid[0]])

def solve_column(args, flow, sponge, coupling):
    source, freq = args
    field = precondition(source, freq, sponge, coupling)
    for sweep in range(SWEEPS):
        padded = jnp.pad(field, ((0, 0), (1, 1), (0, 0), (0, 0), (0, 0)))
        image = apply_adjoint(padded, freq, flow, sponge, coupling)
        field = field + precondition(source - image, freq, sponge, coupling)
    return field

def reference(forcing, flow, sponge, coupling, omega):
    column_ids = jnp.arange(COLS)
    freqs = jnp.where(column_ids < FORCINGS, omega[0], omega[1])
    fields = lax.map(lambda item: solve_column(item, flow, sponge, coupling), (forcing, freqs))
    flat = fields.reshape(COLS, -1)
    total = 2 * NX * V * R * TH
    gram = jnp.dot(flat, flat.T, precision=lax.Precision.HIGHEST)
    lower_factor = jnp.linalg.cholesky(gram)
    inverse = jax.scipy.linalg.solve_triangular(lower_factor, jnp.eye(COLS, dtype=jnp.float32), lower=True)
    basis = jnp.dot(inverse, flat, precision=lax.Precision.HIGHEST) * jnp.sqrt(jnp.float32(total))
    coeff = lower_factor.T / jnp.sqrt(jnp.float32(total))
    return (basis.reshape(forcing.shape), coeff)
```

```python
import functools

import jax
import jax.numpy as jnp
from jax import lax
from jax.experimental import pallas as pl
from jax.experimental.pallas import tpu as pltpu
from jax.sharding import PartitionSpec as P

FORCINGS = 8
SWEEPS = 8

viscosity = 0.25
SUB, LANE = 8, 128
EXACT = lax.Precision.HIGHEST


def fold(plane):
    return jnp.concatenate([plane[:, :LANE], plane[:, LANE:]], axis=0)


def pack_kernel(forcing_ref, sponge_ref, flow_ref, *out_refs):
    cols, parts, planes, nvar = forcing_ref.shape[:4]
    me = lax.rem(lax.axis_index("gx"), cols)
    rows = parts * planes * nvar
    for k, out_ref in enumerate(out_refs):
        col = lax.rem(me + k, cols)
        for part in range(parts):
            for plane in range(planes):
                for v in range(nvar):
                    row = (part * planes + plane) * nvar + v
                    out_ref[row] = fold(forcing_ref[col, part, plane, v])
        for plane in range(planes):
            out_ref[rows + plane] = fold(sponge_ref[plane])
            out_ref[rows + planes + plane] = fold(flow_ref[plane])


def pack(forcing, sponge, flow):
    cols, parts, planes, nvar = forcing.shape[:4]
    rows = planes * (parts * nvar + 2)
    slab = jax.ShapeDtypeStruct((rows, SUB, LANE), jnp.float32)
    return pl.pallas_call(
        pack_kernel,
        out_shape=(slab,) * cols,
        in_specs=[pl.BlockSpec(memory_space=pltpu.VMEM)] * 3,
        out_specs=(pl.BlockSpec(memory_space=pltpu.VMEM),) * cols,
        name="pack",
    )(forcing, sponge, flow)


def locate(i, two_sided, flip, cols, planes, span):
    own = cols * planes
    if two_sided:
        j = i - span
        slab, inner = lax.div(j + span, planes) - span // planes, lax.rem(i, planes)
        slot = jnp.where(slab < 0, slab + 2 * cols, slab)
        return slot, inner, i
    slab, inner = lax.div(i, planes), lax.rem(i, planes)
    far = jnp.where(i < own, cols - 1 - slab, 3 * cols - 1 - slab)
    return jnp.where(flip == 1, far, slab), jnp.where(flip == 1, planes - 1 - inner, inner), i


def sweep_kernel(dims, two_sided, *refs):
    cols, parts, planes, nvar, groups = dims
    coupling_ref, omega_ref = refs[:2]
    slab_refs = refs[2 : 2 + 2 * cols]
    out_ref = refs[2 + 2 * cols]
    raw, first, even, odd, p_re, p_im, w_lo, w_hi, sems = refs[3 + 2 * cols :]
    gx = lax.axis_index("gx")
    me, group = lax.rem(gx, cols), lax.div(gx, cols)
    flip = jnp.int32(0) if two_sided else jnp.int32(group)
    rows = planes * (parts * nvar + 2)
    comp = parts * nvar
    own, span = cols * planes, SWEEPS
    window = own + span * (2 if two_sided else 1)

    copies = []
    for k, slab_ref in enumerate(slab_refs):
        slot = lax.rem(me + cols - k % cols, cols) + cols * (k // cols)
        copies.append(pltpu.make_async_copy(slab_ref, raw.at[pl.ds(slot * rows, rows)], sems.at[k]))
        copies[-1].start()

    column = lax.axis_index("af") * cols + me
    freq = jnp.where(column < FORCINGS, omega_ref[0], omega_ref[1])
    side = jnp.where(flip == 1, -2.0, 2.0).astype(jnp.float32)
    zero = jnp.zeros((SUB, LANE), jnp.float32)
    for ref in (first, even, odd):
        for c in range(comp):
            ref[c] = zero
    for copy in copies:
        copy.wait()

    def prepare(i, _):
        slot, inner, _ = locate(i, two_sided, flip, cols, planes, span)
        base = slot * rows
        sponge = raw[base + planes * comp + inner]
        flow = raw[base + planes * comp + planes + inner]
        w_lo[i] = 1.0 - side * flow
        w_hi[i] = 1.0 + side * flow
        if two_sided:
            inside = jnp.logical_and(
                jnp.logical_or(i >= span, group > 0),
                jnp.logical_or(i < span + own, group < groups - 1),
            )
            keep = jnp.where(inside, 1.0, 0.0).astype(jnp.float32)
        for v in range(nvar):
            diag = sponge + (6.0 * viscosity - coupling_ref[v, v])
            scale = 1.0 / (diag * diag + freq * freq)
            if two_sided:
                scale = scale * keep
            pr, pi = diag * scale, freq * scale
            f_re = raw[base + inner * nvar + v]
            f_im = raw[base + planes * nvar + inner * nvar + v]
            first[(i + 1) * comp + v] = pr * f_re - pi * f_im
            first[(i + 1) * comp + nvar + v] = pr * f_im + pi * f_re
            p_re[i * nvar + v] = viscosity * pr
            p_im[i * nvar + v] = viscosity * pi
        return 0

    lax.fori_loop(0, window, prepare, 0)

    lane = lax.broadcasted_iota(jnp.int32, (SUB, LANE), 1)
    radial = lax.rem(lax.broadcasted_iota(jnp.int32, (SUB, LANE), 0), SUB // 2)
    at_last, at_first = lane == LANE - 1, lane == 0
    at_outer, at_axis = radial == SUB // 2 - 1, radial == 0
    pull = [[coupling_ref[u, v] * (1.0 / viscosity) for v in range(nvar)] for u in range(nvar)]

    def update(i, src, emit):
        field = [src[(i + 1) * comp + c] for c in range(comp)]
        lo, hi = w_lo[i], w_hi[i]
        for v in range(nvar):
            sums = []
            for part in range(parts):
                c = part * nvar + v
                z = field[c]
                other = pltpu.roll(z, SUB // 2, 0)
                total = pltpu.roll(jnp.where(at_last, other, z), 1, 1)
                total = total + pltpu.roll(jnp.where(at_first, other, z), LANE - 1, 1)
                total = total + jnp.where(at_axis, 0.0, pltpu.roll(z, 1, 0))
                total = total + jnp.where(at_outer, 0.0, pltpu.roll(z, SUB - 1, 0))
                total = total + lo * src[i * comp + c]
                total = total + hi * src[(i + 2) * comp + c]
                for u in range(nvar):
                    if u != v:
                        total = total + pull[u][v] * field[part * nvar + u]
                sums.append(total)
            pr, pi = p_re[i * nvar + v], p_im[i * nvar + v]
            emit(i, v, first[(i + 1) * comp + v] + (pr * sums[0] - pi * sums[1]))
            emit(i, nvar + v, first[(i + 1) * comp + nvar + v] + (pr * sums[1] + pi * sums[0]))

    def level(src, emit, lo, hi, unroll):
        def body(n, _):
            for m in range(unroll):
                update(lo + n * unroll + m, src, emit)
            return 0

        trips = (hi - lo) // unroll
        lax.fori_loop(0, trips, body, 0)
        for i in range(lo + trips * unroll, hi):
            update(jnp.int32(i), src, emit)

    def into(ref):
        def emit(i, c, value):
            ref[(i + 1) * comp + c] = value

        return emit

    def finish(i, c, value):
        plane = i - span if two_sided else jnp.where(flip == 1, own - 1 - i, i)
        out_ref[lax.rem(plane, planes) * cols + lax.div(plane, planes), c] = value

    src = first
    for s in range(1, SWEEPS):
        dst = odd if s % 2 else even
        level(src, into(dst), s if two_sided else 0, window - s, 2)
        src = dst
    start = span if two_sided else 0
    level(src, finish, start, start + own, 2)


def sweeps(coupling, omega, slabs, dims, two_sided):
    cols, parts, planes, nvar, groups = dims
    comp = parts * nvar
    rows = planes * (comp + 2)
    own = cols * planes
    window = own + SWEEPS * (2 if two_sided else 1)
    tiles = lambda n: pltpu.VMEM((n, SUB, LANE), jnp.float32)
    return pl.pallas_call(
        functools.partial(sweep_kernel, dims, two_sided),
        out_shape=jax.ShapeDtypeStruct((own, comp, SUB, LANE), jnp.float32),
        in_specs=[pl.BlockSpec(memory_space=pltpu.SMEM)] * 2 + [pl.BlockSpec(memory_space=pl.ANY)] * len(slabs),
        out_specs=pl.BlockSpec(memory_space=pltpu.VMEM),
        scratch_shapes=[
            tiles(2 * cols * rows),
            tiles((window + 2) * comp),
            tiles((window + 2) * comp),
            tiles((window + 2) * comp),
            tiles(window * nvar),
            tiles(window * nvar),
            tiles(window),
            tiles(window),
            pltpu.SemaphoreType.DMA((2 * cols,)),
        ],
        name="sweeps",
    )(coupling, omega, *slabs)


def gram_kernel(y_ref, g_ref):
    count, comp = y_ref.shape[:2]
    rows = count * SUB
    pair = (((1,), (1,)), ((), ()))
    total = jnp.zeros((rows, rows), jnp.float32)
    for c in range(comp):
        part = y_ref[:, c].reshape(rows, LANE)
        total = total + lax.dot_general(part, part, pair, precision=EXACT, preferred_element_type=jnp.float32)
    row = lax.broadcasted_iota(jnp.int32, (rows, rows), 0)
    col = lax.broadcasted_iota(jnp.int32, (rows, rows), 1)
    total = jnp.where(lax.rem(row, SUB) == lax.rem(col, SUB), total, 0.0)
    owner = lax.div(lax.broadcasted_iota(jnp.int32, (count, rows), 1), SUB)
    member = (owner == lax.broadcasted_iota(jnp.int32, (count, rows), 0)).astype(jnp.float32)
    half = lax.dot_general(member, total, (((1,), (0,)), ((), ())), precision=EXACT, preferred_element_type=jnp.float32)
    g_ref[...] = lax.dot_general(half, member, pair, precision=EXACT, preferred_element_type=jnp.float32)


def gram(y):
    return pl.pallas_call(
        gram_kernel,
        out_shape=jax.ShapeDtypeStruct((y.shape[0],) * 2, jnp.float32),
        in_specs=[pl.BlockSpec(memory_space=pltpu.VMEM)],
        out_specs=pl.BlockSpec(memory_space=pltpu.VMEM),
        name="gram",
    )(y)


def factor_kernel(length, g_ref, coeff_ref, linv_ref):
    n = g_ref.shape[0]
    row = lax.broadcasted_iota(jnp.int32, (n, n), 0)
    col = lax.broadcasted_iota(jnp.int32, (n, n), 1)
    left, right = g_ref[...], (row == col).astype(jnp.float32)
    upper, lower = jnp.zeros((n, n), jnp.float32), jnp.zeros((n, n), jnp.float32)
    for k in range(n):
        pivot = left[k : k + 1, k : k + 1]
        left_row, right_row = left[k : k + 1, :], right[k : k + 1, :]
        root = 1.0 / jnp.sqrt(pivot)
        upper = jnp.where(row == k, left_row * root, upper)
        lower = jnp.where(row == k, right_row * root, lower)
        times = jnp.where(row > k, left[:, k : k + 1] / pivot, 0.0)
        left = left - times * left_row
        right = right - times * right_row
    coeff_ref[...] = jnp.where(col >= row, upper, 0.0) / jnp.sqrt(jnp.float32(length))
    linv_ref[...] = lower * jnp.sqrt(jnp.float32(length))


def factor(g, length):
    square = jax.ShapeDtypeStruct(g.shape, jnp.float32)
    return pl.pallas_call(
        functools.partial(factor_kernel, length),
        out_shape=(square, square),
        in_specs=[pl.BlockSpec(memory_space=pltpu.VMEM)],
        out_specs=(pl.BlockSpec(memory_space=pltpu.VMEM),) * 2,
        name="factor",
    )(g)


def basis_kernel(linv_ref, *refs):
    y_refs, out_ref, table = refs[:-2], refs[-2], refs[-1]
    cols, parts, planes, nvar = out_ref.shape[:4]
    count = linv_ref.shape[0]
    af = lax.axis_index("af")
    for c in range(cols):
        line = linv_ref[pl.ds(af * cols + c, 1), :]
        for u in range(count):
            table[c * count + u] = jnp.broadcast_to(line[:, u : u + 1], (SUB, LANE))
    for k, y_ref in enumerate(y_refs):
        plane = lax.bitwise_xor(af, k)
        for part in range(parts):
            sums = [[None] * nvar for _ in range(cols)]
            for u in range(count):
                values = [y_ref[u, part * nvar + v] for v in range(nvar)]
                for c in range(cols):
                    times = table[c * count + u]
                    for v in range(nvar):
                        term = times * values[v]
                        sums[c][v] = term if u == 0 else sums[c][v] + term
            for c in range(cols):
                for v in range(nvar):
                    out_ref[c, part, plane, v, :, :LANE] = sums[c][v][: SUB // 2]
                    out_ref[c, part, plane, v, :, LANE:] = sums[c][v][SUB // 2 :]


def basis_of(linv, ys, shape):
    return pl.pallas_call(
        basis_kernel,
        out_shape=jax.ShapeDtypeStruct(shape, jnp.float32),
        in_specs=[pl.BlockSpec(memory_space=pltpu.VMEM)] * (1 + len(ys)),
        out_specs=pl.BlockSpec(memory_space=pltpu.VMEM),
        scratch_shapes=[pltpu.VMEM((shape[0] * linv.shape[0], SUB, LANE), jnp.float32)],
        name="basis",
    )(linv, *ys)


def on_device(size_x, size_f, forcing, flow, sponge, coupling, omega):
    cols, parts, planes, nvar, rad, azi = forcing.shape
    groups = size_x // cols
    two_sided = groups != 2
    count = cols * size_f
    assert rad * azi == SUB * LANE and azi == 2 * LANE and size_x % cols == 0
    assert planes == size_f and 2 * planes == SWEEPS and cols == 4
    dims = (cols, parts, planes, nvar, groups)

    slabs = pack(forcing, sponge, flow)
    halo = []
    for k in range(cols):
        pairs = []
        for g in range(size_x):
            group, j = divmod(g, cols)
            target = group - 1 if j < cols // 2 else group + 1
            if 0 <= target < groups:
                pairs.append((g, target * cols + (j + k) % cols))
        halo.append(lax.ppermute(slabs[k], "gx", pairs))
    mine = [slabs[0]]
    for k in range(1, cols):
        pairs = [(g, g // cols * cols + (g + k) % cols) for g in range(size_x)]
        mine.append(lax.ppermute(slabs[k], "gx", pairs))
    z = sweeps(coupling, omega, mine + halo, dims, two_sided)

    together = [
        [(q * cols + j) * size_f + a for a in range(size_f) for j in range(cols)] for q in range(groups)
    ]
    y = lax.all_to_all(z, ("gx", "af"), 0, 0, axis_index_groups=together, tiled=True)
    ys = [y] + [None] * (size_f - 1)
    ys[2] = lax.ppermute(y, "af", [(a, a ^ 2) for a in range(size_f)])
    ys[1] = lax.ppermute(y, "af", [(a, a ^ 1) for a in range(size_f)])
    ys[3] = lax.ppermute(ys[2], "af", [(a, a ^ 1) for a in range(size_f)])
    g = gram(y)
    step = 1
    while step < size_f:
        g = g + lax.ppermute(g, "af", [(a, a ^ step) for a in range(size_f)])
        step *= 2
    step = 1
    while step < size_x:
        g = g + lax.ppermute(g, "gx", [(a, a ^ step) for a in range(size_x)])
        step *= 2
    length = parts * planes * nvar * rad * azi * size_x
    coeff, linv = factor(g, length)
    return basis_of(linv, ys, forcing.shape), coeff


def solution(mesh):
    placed = (
        P("af", None, "gx", None, None, None),
        P("gx", None, None),
        P("gx", None, None),
        P(),
        P(),
    )
    return jax.shard_map(
        functools.partial(on_device, mesh.shape["gx"], mesh.shape["af"]),
        mesh=mesh,
        in_specs=placed,
        out_specs=(P("af", None, "gx", None, None, None), P()),
        check_vma=False,
    )
```

```python
import functools

import jax
import jax.numpy as jnp
from jax import lax
from jax.experimental import pallas as pl
from jax.experimental.pallas import tpu as pltpu
from jax.sharding import PartitionSpec as P

FORCINGS = 8
SWEEPS = 8

viscosity = 0.25
SUB, LANE = 8, 128
EXACT = lax.Precision.HIGHEST


def fold(plane):
    return jnp.concatenate([plane[:, :LANE], plane[:, LANE:]], axis=0)


def pack_kernel(forcing_hbm, sponge_hbm, flow_hbm, *refs):
    cols, parts, planes, nvar = forcing_hbm.shape[:4]
    out_refs, (forcing_ref, sponge_ref, flow_ref, sems) = refs[:cols], refs[cols:]
    me = lax.rem(lax.axis_index("gx"), cols)
    rows = parts * planes * nvar
    copies = []
    for k in range(cols):
        col = lax.rem(me + k, cols)
        copies.append(pltpu.make_async_copy(forcing_hbm.at[col], forcing_ref.at[k], sems.at[k]))
    copies.append(pltpu.make_async_copy(sponge_hbm, sponge_ref, sems.at[cols]))
    copies.append(pltpu.make_async_copy(flow_hbm, flow_ref, sems.at[cols + 1]))
    for copy in copies:
        copy.start()
    for copy in copies[cols:]:
        copy.wait()
    for plane in range(planes):
        sponge, flow = fold(sponge_ref[plane]), fold(flow_ref[plane])
        for out_ref in out_refs:
            out_ref[rows + plane] = sponge
            out_ref[rows + planes + plane] = flow
    for k, out_ref in enumerate(out_refs):
        copies[k].wait()
        for part in range(parts):
            for plane in range(planes):
                for v in range(nvar):
                    row = (part * planes + plane) * nvar + v
                    out_ref[row] = fold(forcing_ref[k, part, plane, v])


def pack(forcing, sponge, flow):
    cols, parts, planes, nvar = forcing.shape[:4]
    rows = planes * (parts * nvar + 2)
    slab = jax.ShapeDtypeStruct((rows, SUB, LANE), jnp.float32)
    return pl.pallas_call(
        pack_kernel,
        out_shape=(slab,) * cols,
        in_specs=[pl.BlockSpec(memory_space=pltpu.HBM)] * 3,
        out_specs=(pl.BlockSpec(memory_space=pltpu.VMEM),) * cols,
        scratch_shapes=[
            pltpu.VMEM(forcing.shape, jnp.float32),
            pltpu.VMEM(sponge.shape, jnp.float32),
            pltpu.VMEM(flow.shape, jnp.float32),
            pltpu.SemaphoreType.DMA((cols + 2,)),
        ],
        compiler_params=pltpu.CompilerParams(vmem_limit_bytes=4 << 20),
        name="pack",
    )(forcing, sponge, flow)


def sweep_kernel(dims, two_sided, outer, *refs):
    cols, parts, planes, nvar, groups = dims
    comp = parts * nvar
    state = 8
    coupling_hbm, omega_hbm = refs[:2]
    slab_refs = refs[2 : 2 + cols]
    at = 2 + cols + (state if outer else 0)
    out_ref, first, even, odd, p_re, p_im, w_lo, w_hi = refs[at : at + state]
    raw, coupling_ref, omega_ref, sems = refs[at + state :]
    gx = lax.axis_index("gx")
    me, group = lax.rem(gx, cols), lax.div(gx, cols)
    flip = jnp.int32(0) if two_sided else jnp.int32(group)
    rows = planes * (comp + 2)
    own, span = cols * planes, SWEEPS
    begin = span if two_sided else 0
    end = begin + own
    window = end + span

    scalars = [
        pltpu.make_async_copy(coupling_hbm, coupling_ref, sems.at[cols]),
        pltpu.make_async_copy(omega_hbm, omega_ref, sems.at[cols + 1]),
    ]
    for copy in scalars:
        copy.start()
    copies = []
    for k, slab_ref in enumerate(slab_refs):
        slot = lax.rem(me + cols - k, cols)
        copies.append(pltpu.make_async_copy(slab_ref, raw.at[pl.ds(slot * rows, rows)], sems.at[k]))
        copies[-1].start()

    for copy in scalars:
        copy.wait()
    column = lax.axis_index("af") * cols + me
    freq = jnp.where(column < FORCINGS, omega_ref[0], omega_ref[1])
    side = jnp.where(flip == 1, -2.0, 2.0).astype(jnp.float32)
    if not outer:
        for ref in (first, even, odd):
            for c in range(comp):
                ref[c] = jnp.zeros((SUB, LANE), jnp.float32)
    for copy in copies:
        copy.wait()

    def prepare(i, _):
        slab, inner = lax.div(i - begin + span, planes) - span // planes, lax.rem(i, planes)
        if two_sided:
            slot = jnp.where(slab < 0, slab + cols, lax.rem(slab, cols))
            inside = jnp.logical_and(
                jnp.logical_or(i >= begin, group > 0), jnp.logical_or(i < end, group < groups - 1)
            )
            keep = jnp.where(inside, 1.0, 0.0).astype(jnp.float32)
        else:
            slot = lax.rem(slab, cols)
            slot = jnp.where(flip == 1, cols - 1 - slot, slot)
            inner = jnp.where(flip == 1, planes - 1 - inner, inner)
        base = slot * rows
        sponge = raw[base + planes * comp + inner]
        flow = raw[base + planes * comp + planes + inner]
        w_lo[i] = 1.0 - side * flow
        w_hi[i] = 1.0 + side * flow
        for v in range(nvar):
            diag = sponge + (6.0 * viscosity - coupling_ref[v, v])
            scale = 1.0 / (diag * diag + freq * freq)
            if two_sided:
                scale = scale * keep
            pr, pi = diag * scale, freq * scale
            f_re = raw[base + inner * nvar + v]
            f_im = raw[base + planes * nvar + inner * nvar + v]
            first[(i + 1) * comp + v] = pr * f_re - pi * f_im
            first[(i + 1) * comp + nvar + v] = pr * f_im + pi * f_re
            p_re[i * nvar + v] = viscosity * pr
            p_im[i * nvar + v] = viscosity * pi
        return 0

    if outer:
        lax.fori_loop(end, window, prepare, 0)
        if two_sided:
            lax.fori_loop(0, begin, prepare, 0)
    else:
        lax.fori_loop(begin, end, prepare, 0)

    lane = lax.broadcasted_iota(jnp.int32, (SUB, LANE), 1)
    radial = lax.rem(lax.broadcasted_iota(jnp.int32, (SUB, LANE), 0), SUB // 2)
    at_last, at_first = lane == LANE - 1, lane == 0
    at_outer, at_axis = radial == SUB // 2 - 1, radial == 0
    pull = [[coupling_ref[u, v] * (1.0 / viscosity) for v in range(nvar)] for u in range(nvar)]

    def update(i, src, emit):
        field = [src[(i + 1) * comp + c] for c in range(comp)]
        lo, hi = w_lo[i], w_hi[i]
        for v in range(nvar):
            sums = []
            for part in range(parts):
                c = part * nvar + v
                z = field[c]
                other = pltpu.roll(z, SUB // 2, 0)
                total = pltpu.roll(jnp.where(at_last, other, z), 1, 1)
                total = total + pltpu.roll(jnp.where(at_first, other, z), LANE - 1, 1)
                total = total + jnp.where(at_axis, 0.0, pltpu.roll(z, 1, 0))
                total = total + jnp.where(at_outer, 0.0, pltpu.roll(z, SUB - 1, 0))
                total = total + lo * src[i * comp + c]
                total = total + hi * src[(i + 2) * comp + c]
                for u in range(nvar):
                    if u != v:
                        total = total + pull[u][v] * field[part * nvar + u]
                sums.append(total)
            pr, pi = p_re[i * nvar + v], p_im[i * nvar + v]
            emit(i, v, first[(i + 1) * comp + v] + (pr * sums[0] - pi * sums[1]))
            emit(i, nvar + v, first[(i + 1) * comp + nvar + v] + (pr * sums[1] + pi * sums[0]))

    def level(src, emit, lo, hi, unroll=2):
        def body(n, _):
            for m in range(unroll):
                update(lo + n * unroll + m, src, emit)
            return 0

        trips = (hi - lo) // unroll
        lax.fori_loop(0, trips, body, 0)
        for i in range(lo + trips * unroll, hi):
            update(jnp.int32(i), src, emit)

    def into(ref):
        def emit(i, c, value):
            ref[(i + 1) * comp + c] = value

        return emit

    def finish(i, c, value):
        plane = i - begin if two_sided else jnp.where(flip == 1, own - 1 - i, i)
        out_ref[lax.rem(plane, planes) * cols + lax.div(plane, planes), c] = value

    src = first
    for s in range(1, SWEEPS + 1):
        dst = odd if s % 2 else even
        emit = finish if s == SWEEPS else into(dst)
        if outer:
            if two_sided:
                level(src, emit, s, begin + s)
            level(src, emit, end - s, window - s)
        else:
            level(src, emit, begin + s if two_sided else 0, end - s)
        src = dst


def sweeps(coupling, omega, slabs, dims, two_sided, state=()):
    cols, parts, planes, nvar, groups = dims
    comp = parts * nvar
    own = cols * planes
    window = own + SWEEPS * (2 if two_sided else 1)
    tiles = lambda n: jax.ShapeDtypeStruct((n, SUB, LANE), jnp.float32)
    shapes = [jax.ShapeDtypeStruct((own, comp, SUB, LANE), jnp.float32)]
    shapes += [tiles((window + 2) * comp)] * 3 + [tiles(window * nvar)] * 2 + [tiles(window)] * 2
    fast = pl.BlockSpec(memory_space=pltpu.VMEM)
    lead = 2 + len(slabs)
    return pl.pallas_call(
        functools.partial(sweep_kernel, dims, two_sided, bool(state)),
        out_shape=shapes,
        in_specs=[pl.BlockSpec(memory_space=pltpu.HBM)] * 2
        + [pl.BlockSpec(memory_space=pl.ANY)] * len(slabs)
        + [fast] * len(state),
        out_specs=[fast] * len(shapes),
        scratch_shapes=[
            pltpu.VMEM((cols * planes * (comp + 2), SUB, LANE), jnp.float32),
            pltpu.SMEM(coupling.shape, jnp.float32),
            pltpu.SMEM(omega.shape, jnp.float32),
            pltpu.SemaphoreType.DMA((cols + 2,)),
        ],
        input_output_aliases={lead + n: n for n in range(len(state))},
        compiler_params=pltpu.CompilerParams(vmem_limit_bytes=16 << 20),
        cost_estimate=pl.CostEstimate(flops=6_000_000_000, bytes_accessed=1 << 20, transcendentals=0),
        name="outer" if state else "inner",
    )(coupling, omega, *slabs, *state)


def gram_kernel(y_ref, g_ref):
    count, comp = y_ref.shape[:2]
    rows = count * SUB
    pair = (((1,), (1,)), ((), ()))
    total = jnp.zeros((rows, rows), jnp.float32)
    for c in range(comp):
        part = y_ref[:, c].reshape(rows, LANE)
        total = total + lax.dot_general(part, part, pair, precision=EXACT, preferred_element_type=jnp.float32)
    row = lax.broadcasted_iota(jnp.int32, (rows, rows), 0)
    col = lax.broadcasted_iota(jnp.int32, (rows, rows), 1)
    total = jnp.where(lax.rem(row, SUB) == lax.rem(col, SUB), total, 0.0)
    owner = lax.div(lax.broadcasted_iota(jnp.int32, (count, rows), 1), SUB)
    member = (owner == lax.broadcasted_iota(jnp.int32, (count, rows), 0)).astype(jnp.float32)
    half = lax.dot_general(member, total, (((1,), (0,)), ((), ())), precision=EXACT, preferred_element_type=jnp.float32)
    g_ref[...] = lax.dot_general(half, member, pair, precision=EXACT, preferred_element_type=jnp.float32)


def gram(y):
    return pl.pallas_call(
        gram_kernel,
        out_shape=jax.ShapeDtypeStruct((y.shape[0],) * 2, jnp.float32),
        in_specs=[pl.BlockSpec(memory_space=pltpu.VMEM)],
        out_specs=pl.BlockSpec(memory_space=pltpu.VMEM),
        compiler_params=pltpu.CompilerParams(vmem_limit_bytes=4 << 20),
        cost_estimate=pl.CostEstimate(flops=2_000_000_000, bytes_accessed=1 << 20, transcendentals=0),
        name="gram",
    )(y)


def factor_kernel(length, g_ref, coeff_ref, linv_ref):
    n = g_ref.shape[0]
    row = lax.broadcasted_iota(jnp.int32, (n, n), 0)
    col = lax.broadcasted_iota(jnp.int32, (n, n), 1)
    left, right = g_ref[...], (row == col).astype(jnp.float32)
    upper, lower = jnp.zeros((n, n), jnp.float32), jnp.zeros((n, n), jnp.float32)
    for k in range(n):
        pivot = left[k : k + 1, k : k + 1]
        left_row, right_row = left[k : k + 1, :], right[k : k + 1, :]
        root = 1.0 / jnp.sqrt(pivot)
        upper = jnp.where(row == k, left_row * root, upper)
        lower = jnp.where(row == k, right_row * root, lower)
        times = jnp.where(row > k, left[:, k : k + 1] / pivot, 0.0)
        left = left - times * left_row
        right = right - times * right_row
    coeff_ref[...] = jnp.where(col >= row, upper, 0.0) / jnp.sqrt(jnp.float32(length))
    linv_ref[...] = lower * jnp.sqrt(jnp.float32(length))


def factor(g, length):
    square = jax.ShapeDtypeStruct(g.shape, jnp.float32)
    return pl.pallas_call(
        functools.partial(factor_kernel, length),
        out_shape=(square, square),
        in_specs=[pl.BlockSpec(memory_space=pltpu.VMEM)],
        out_specs=(pl.BlockSpec(memory_space=pltpu.VMEM),) * 2,
        compiler_params=pltpu.CompilerParams(vmem_limit_bytes=1 << 20),
        name="factor",
    )(g)


def basis_kernel(linv_ref, *refs):
    y_refs, out_ref, table = refs[:-2], refs[-2], refs[-1]
    cols, parts, planes, nvar = out_ref.shape[:4]
    count = linv_ref.shape[0]
    af = lax.axis_index("af")
    for c in range(cols):
        line = linv_ref[pl.ds(af * cols + c, 1), :]
        for u in range(count):
            table[c * count + u] = jnp.broadcast_to(line[:, u : u + 1], (SUB, LANE))
    for k, y_ref in enumerate(y_refs):
        plane = lax.bitwise_xor(af, k)
        for part in range(parts):
            sums = [[None] * nvar for _ in range(cols)]
            for u in range(count):
                values = [y_ref[u, part * nvar + v] for v in range(nvar)]
                for c in range(cols):
                    times = table[c * count + u]
                    for v in range(nvar):
                        term = times * values[v]
                        sums[c][v] = term if u == 0 else sums[c][v] + term
            for c in range(cols):
                for v in range(nvar):
                    out_ref[c, part, plane, v, :, :LANE] = sums[c][v][: SUB // 2]
                    out_ref[c, part, plane, v, :, LANE:] = sums[c][v][SUB // 2 :]


def basis_of(linv, ys, shape):
    return pl.pallas_call(
        basis_kernel,
        out_shape=jax.ShapeDtypeStruct(shape, jnp.float32),
        in_specs=[pl.BlockSpec(memory_space=pltpu.VMEM)] * (1 + len(ys)),
        out_specs=pl.BlockSpec(memory_space=pltpu.VMEM),
        scratch_shapes=[pltpu.VMEM((shape[0] * linv.shape[0], SUB, LANE), jnp.float32)],
        compiler_params=pltpu.CompilerParams(vmem_limit_bytes=8 << 20),
        name="basis",
    )(linv, *ys)


def on_device(size_x, size_f, forcing, flow, sponge, coupling, omega):
    cols, parts, planes, nvar, rad, azi = forcing.shape
    groups = size_x // cols
    two_sided = groups != 2
    count = cols * size_f
    assert rad * azi == SUB * LANE and azi == 2 * LANE and size_x % cols == 0
    assert planes == size_f and 2 * planes == SWEEPS and cols == 4
    dims = (cols, parts, planes, nvar, groups)

    slabs = pack(forcing, sponge, flow)
    halo = []
    for k in range(cols):
        pairs = []
        for g in range(size_x):
            group, j = divmod(g, cols)
            target = group - 1 if j < cols // 2 else group + 1
            if 0 <= target < groups:
                pairs.append((g, target * cols + (j + k) % cols))
        halo.append(lax.ppermute(slabs[k], "gx", pairs))
    mine = [slabs[0]]
    for k in range(1, cols):
        pairs = [(g, g // cols * cols + (g + k) % cols) for g in range(size_x)]
        mine.append(lax.ppermute(slabs[k], "gx", pairs))
    state = sweeps(coupling, omega, mine, dims, two_sided)
    z = sweeps(coupling, omega, halo, dims, two_sided, state)[0]

    together = [
        [(q * cols + j) * size_f + a for a in range(size_f) for j in range(cols)] for q in range(groups)
    ]
    y = lax.all_to_all(z, ("gx", "af"), 0, 0, axis_index_groups=together, tiled=True)
    ys = [y] + [None] * (size_f - 1)
    ys[2] = lax.ppermute(y, "af", [(a, a ^ 2) for a in range(size_f)])
    ys[1] = lax.ppermute(y, "af", [(a, a ^ 1) for a in range(size_f)])
    g = gram(y)
    step = 1
    while step < size_x:
        g = g + lax.ppermute(g, "gx", [(a, a ^ step) for a in range(size_x)])
        step *= 2
    g = g + lax.ppermute(g, "af", [(a, a ^ 1) for a in range(size_f)])
    g, ys[2] = lax.optimization_barrier((g, ys[2]))
    g = g + lax.ppermute(g, "af", [(a, a ^ 2) for a in range(size_f)])
    ys[3] = lax.ppermute(ys[2], "af", [(a, a ^ 1) for a in range(size_f)])
    length = parts * planes * nvar * rad * azi * size_x
    coeff, linv = factor(g, length)
    return basis_of(linv, ys, forcing.shape), coeff


def solution(mesh):
    placed = (
        P("af", None, "gx", None, None, None),
        P("gx", None, None),
        P("gx", None, None),
        P(),
        P(),
    )
    return jax.shard_map(
        functools.partial(on_device, mesh.shape["gx"], mesh.shape["af"]),
        mesh=mesh,
        in_specs=placed,
        out_specs=(P("af", None, "gx", None, None, None), P()),
        check_vma=False,
    )
```

```python
import functools

import jax
import jax.numpy as jnp
from jax import lax
from jax.experimental import pallas as pl
from jax.experimental.pallas import tpu as pltpu
from jax.sharding import PartitionSpec as P


FORCINGS = 8
SWEEPS = 8

viscosity = 0.25
SUB, LANE = 8, 128
EXACT = lax.Precision.HIGHEST


def fold(plane):
    return jnp.concatenate([plane[:, :LANE], plane[:, LANE:]], axis=0)


def pack_kernel(forcing_hbm, sponge_hbm, flow_hbm, *refs):
    cols, parts, planes, nvar = forcing_hbm.shape[:4]
    out_refs, (forcing_ref, sponge_ref, flow_ref, sems) = refs[:cols], refs[cols:]
    me = lax.rem(lax.axis_index("gx"), cols)
    rows = parts * planes * nvar
    copies = []
    for k in range(cols):
        col = lax.bitwise_xor(me, k)
        copies.append(pltpu.make_async_copy(forcing_hbm.at[col], forcing_ref.at[k], sems.at[k]))
    copies.append(pltpu.make_async_copy(sponge_hbm, sponge_ref, sems.at[cols]))
    copies.append(pltpu.make_async_copy(flow_hbm, flow_ref, sems.at[cols + 1]))
    for copy in copies:
        copy.start()
    for copy in copies[cols:]:
        copy.wait()
    for plane in range(planes):
        sponge, flow = fold(sponge_ref[plane]), fold(flow_ref[plane])
        for out_ref in out_refs:
            out_ref[rows + plane] = sponge
            out_ref[rows + planes + plane] = flow
    for k, out_ref in enumerate(out_refs):
        copies[k].wait()
        for part in range(parts):
            for plane in range(planes):
                for v in range(nvar):
                    row = (part * planes + plane) * nvar + v
                    out_ref[row] = fold(forcing_ref[k, part, plane, v])


def in_place(*arrays):
    return tuple(pltpu.with_memory_space_constraint(a, pltpu.HBM) for a in arrays)


def pack(forcing, sponge, flow):
    cols, parts, planes, nvar = forcing.shape[:4]
    rows = planes * (parts * nvar + 2)
    slab = jax.ShapeDtypeStruct((rows, SUB, LANE), jnp.float32)
    return pl.pallas_call(
        pack_kernel,
        out_shape=(slab,) * cols,
        in_specs=[pl.BlockSpec(memory_space=pltpu.HBM)] * 3,
        out_specs=(pl.BlockSpec(memory_space=pltpu.VMEM),) * cols,
        scratch_shapes=[
            pltpu.VMEM(forcing.shape, jnp.float32),
            pltpu.VMEM(sponge.shape, jnp.float32),
            pltpu.VMEM(flow.shape, jnp.float32),
            pltpu.SemaphoreType.DMA((cols + 2,)),
        ],
        compiler_params=pltpu.CompilerParams(vmem_limit_bytes=4 << 20),
        name="pack",
    )(*in_place(forcing, sponge, flow))


def sweep_kernel(dims, two_sided, outer, *refs):
    cols, parts, planes, nvar, groups = dims
    comp = parts * nvar
    state = 8
    coupling_hbm, omega_hbm = refs[:2]
    slab_refs = refs[2 : 2 + cols]
    at = 2 + cols + (state if outer else 0)
    out_ref, first, even, odd, p_re, p_im, w_lo, w_hi = refs[at : at + state]
    raw, coupling_ref, omega_ref, sems = refs[at + state :]
    gx = lax.axis_index("gx")
    me, group = lax.rem(gx, cols), lax.div(gx, cols)
    flip = jnp.int32(0) if two_sided else jnp.int32(group)
    rows = planes * (comp + 2)
    own, span = cols * planes, SWEEPS
    begin = span if two_sided else 0
    end = begin + own
    window = end + span

    scalars = [
        pltpu.make_async_copy(coupling_hbm, coupling_ref, sems.at[cols]),
        pltpu.make_async_copy(omega_hbm, omega_ref, sems.at[cols + 1]),
    ]
    for copy in scalars:
        copy.start()
    copies = []
    for k, slab_ref in enumerate(slab_refs):
        slot = lax.bitwise_xor(me, k)
        copies.append(pltpu.make_async_copy(slab_ref, raw.at[pl.ds(slot * rows, rows)], sems.at[k]))
        copies[-1].start()

    for copy in scalars:
        copy.wait()
    column = lax.axis_index("af") * cols + me
    freq = jnp.where(column < FORCINGS, omega_ref[0], omega_ref[1])
    side = jnp.where(flip == 1, -2.0, 2.0).astype(jnp.float32)
    if not outer:
        for ref in (first, even, odd):
            for c in range(comp):
                ref[c] = jnp.zeros((SUB, LANE), jnp.float32)
    for copy in copies:
        copy.wait()

    def prepare(i, _):
        slab, inner = lax.div(i - begin + span, planes) - span // planes, lax.rem(i, planes)
        if two_sided:
            slot = jnp.where(slab < 0, slab + cols, lax.rem(slab, cols))
            inside = jnp.logical_and(
                jnp.logical_or(i >= begin, group > 0), jnp.logical_or(i < end, group < groups - 1)
            )
            keep = jnp.where(inside, 1.0, 0.0).astype(jnp.float32)
        else:
            slot = lax.rem(slab, cols)
            slot = jnp.where(flip == 1, cols - 1 - slot, slot)
            inner = jnp.where(flip == 1, planes - 1 - inner, inner)
        base = slot * rows
        sponge = raw[base + planes * comp + inner]
        flow = raw[base + planes * comp + planes + inner]
        w_lo[i] = 1.0 - side * flow
        w_hi[i] = 1.0 + side * flow
        for v in range(nvar):
            diag = sponge + (6.0 * viscosity - coupling_ref[v, v])
            scale = 1.0 / (diag * diag + freq * freq)
            if two_sided:
                scale = scale * keep
            pr, pi = diag * scale, freq * scale
            f_re = raw[base + inner * nvar + v]
            f_im = raw[base + planes * nvar + inner * nvar + v]
            first[(i + 1) * comp + v] = pr * f_re - pi * f_im
            first[(i + 1) * comp + nvar + v] = pr * f_im + pi * f_re
            p_re[i * nvar + v] = viscosity * pr
            p_im[i * nvar + v] = viscosity * pi
        return 0

    if outer:
        lax.fori_loop(end, window, prepare, 0)
        if two_sided:
            lax.fori_loop(0, begin, prepare, 0)
    else:
        lax.fori_loop(begin, end, prepare, 0)

    lane = lax.broadcasted_iota(jnp.int32, (SUB, LANE), 1)
    radial = lax.rem(lax.broadcasted_iota(jnp.int32, (SUB, LANE), 0), SUB // 2)
    at_last, at_first = lane == LANE - 1, lane == 0
    at_outer, at_axis = radial == SUB // 2 - 1, radial == 0
    pull = [[coupling_ref[u, v] * (1.0 / viscosity) for v in range(nvar)] for u in range(nvar)]

    def update(i, src, emit):
        field = [src[(i + 1) * comp + c] for c in range(comp)]
        lo, hi = w_lo[i], w_hi[i]
        for v in range(nvar):
            sums = []
            for part in range(parts):
                c = part * nvar + v
                z = field[c]
                other = pltpu.roll(z, SUB // 2, 0)
                total = pltpu.roll(jnp.where(at_last, other, z), 1, 1)
                total = total + pltpu.roll(jnp.where(at_first, other, z), LANE - 1, 1)
                total = total + jnp.where(at_axis, 0.0, pltpu.roll(z, 1, 0))
                total = total + jnp.where(at_outer, 0.0, pltpu.roll(z, SUB - 1, 0))
                total = total + lo * src[i * comp + c]
                total = total + hi * src[(i + 2) * comp + c]
                for u in range(nvar):
                    if u != v:
                        total = total + pull[u][v] * field[part * nvar + u]
                sums.append(total)
            pr, pi = p_re[i * nvar + v], p_im[i * nvar + v]
            emit(i, v, first[(i + 1) * comp + v] + (pr * sums[0] - pi * sums[1]))
            emit(i, nvar + v, first[(i + 1) * comp + nvar + v] + (pr * sums[1] + pi * sums[0]))

    def level(src, emit, lo, hi, unroll=2):
        def body(n, _):
            for m in range(unroll):
                update(lo + n * unroll + m, src, emit)
            return 0

        trips = (hi - lo) // unroll
        lax.fori_loop(0, trips, body, 0)
        for i in range(lo + trips * unroll, hi):
            update(jnp.int32(i), src, emit)

    def into(ref):
        def emit(i, c, value):
            ref[(i + 1) * comp + c] = value

        return emit

    def finish(i, c, value):
        plane = i - begin if two_sided else jnp.where(flip == 1, own - 1 - i, i)
        out_ref[lax.rem(plane, planes) * cols + lax.div(plane, planes), c] = value

    src = first
    for s in range(1, SWEEPS + 1):
        dst = odd if s % 2 else even
        emit = finish if s == SWEEPS else into(dst)
        if outer:
            if two_sided:
                level(src, emit, s, begin + s)
            level(src, emit, end - s, window - s)
        else:
            level(src, emit, begin + s if two_sided else 0, end - s)
        src = dst


def sweeps(coupling, omega, slabs, dims, two_sided, state=()):
    cols, parts, planes, nvar, _ = dims
    comp = parts * nvar
    own = cols * planes
    window = own + SWEEPS * (2 if two_sided else 1)
    tiles = lambda n: jax.ShapeDtypeStruct((n, SUB, LANE), jnp.float32)
    shapes = [jax.ShapeDtypeStruct((own, comp, SUB, LANE), jnp.float32)]
    shapes += [tiles((window + 2) * comp)] * 3 + [tiles(window * nvar)] * 2 + [tiles(window)] * 2
    fast = pl.BlockSpec(memory_space=pltpu.VMEM)
    lead = 2 + len(slabs)
    return pl.pallas_call(
        functools.partial(sweep_kernel, dims, two_sided, bool(state)),
        out_shape=shapes,
        in_specs=[pl.BlockSpec(memory_space=pltpu.HBM)] * 2
        + [pl.BlockSpec(memory_space=pl.ANY)] * len(slabs)
        + [fast] * len(state),
        out_specs=[fast] * len(shapes),
        scratch_shapes=[
            pltpu.VMEM((cols * planes * (comp + 2), SUB, LANE), jnp.float32),
            pltpu.SMEM(coupling.shape, jnp.float32),
            pltpu.SMEM(omega.shape, jnp.float32),
            pltpu.SemaphoreType.DMA((cols + 2,)),
        ],
        input_output_aliases={lead + n: n for n in range(len(state))},
        compiler_params=pltpu.CompilerParams(vmem_limit_bytes=16 << 20),
        cost_estimate=pl.CostEstimate(flops=6_000_000_000, bytes_accessed=1 << 20, transcendentals=0),
        name="outer" if state else "inner",
    )(*in_place(coupling, omega), *slabs, *state)


def gram_kernel(y_ref, g_ref):
    count, comp = y_ref.shape[:2]
    rows = count * SUB
    pair = (((1,), (1,)), ((), ()))
    total = jnp.zeros((rows, rows), jnp.float32)
    for c in range(comp):
        part = y_ref[:, c].reshape(rows, LANE)
        total = total + lax.dot_general(part, part, pair, precision=EXACT, preferred_element_type=jnp.float32)
    row = lax.broadcasted_iota(jnp.int32, (rows, rows), 0)
    col = lax.broadcasted_iota(jnp.int32, (rows, rows), 1)
    total = jnp.where(lax.rem(row, SUB) == lax.rem(col, SUB), total, 0.0)
    owner = lax.div(lax.broadcasted_iota(jnp.int32, (count, rows), 1), SUB)
    member = (owner == lax.broadcasted_iota(jnp.int32, (count, rows), 0)).astype(jnp.float32)
    half = lax.dot_general(member, total, (((1,), (0,)), ((), ())), precision=EXACT, preferred_element_type=jnp.float32)
    g_ref[...] = lax.dot_general(half, member, pair, precision=EXACT, preferred_element_type=jnp.float32)


def gram(y):
    return pl.pallas_call(
        gram_kernel,
        out_shape=jax.ShapeDtypeStruct((y.shape[0],) * 2, jnp.float32),
        in_specs=[pl.BlockSpec(memory_space=pltpu.VMEM)],
        out_specs=pl.BlockSpec(memory_space=pltpu.VMEM),
        compiler_params=pltpu.CompilerParams(vmem_limit_bytes=4 << 20),
        cost_estimate=pl.CostEstimate(flops=2_000_000_000, bytes_accessed=1 << 20, transcendentals=0),
        name="gram",
    )(y)


def factor_kernel(length, g_ref, coeff_ref, linv_ref):
    n = g_ref.shape[0]
    row = lax.broadcasted_iota(jnp.int32, (n, n), 0)
    col = lax.broadcasted_iota(jnp.int32, (n, n), 1)
    left, right = g_ref[...], (row == col).astype(jnp.float32)
    upper, lower = jnp.zeros((n, n), jnp.float32), jnp.zeros((n, n), jnp.float32)
    for k in range(n):
        pivot = left[k : k + 1, k : k + 1]
        left_row, right_row = left[k : k + 1, :], right[k : k + 1, :]
        root = 1.0 / jnp.sqrt(pivot)
        upper = jnp.where(row == k, left_row * root, upper)
        lower = jnp.where(row == k, right_row * root, lower)
        times = jnp.where(row > k, left[:, k : k + 1] / pivot, 0.0)
        left = left - times * left_row
        right = right - times * right_row
    coeff_ref[...] = jnp.where(col >= row, upper, 0.0) / jnp.sqrt(jnp.float32(length))
    linv_ref[...] = lower * jnp.sqrt(jnp.float32(length))


def factor(g, length):
    square = jax.ShapeDtypeStruct(g.shape, jnp.float32)
    return pl.pallas_call(
        functools.partial(factor_kernel, length),
        out_shape=(square, square),
        in_specs=[pl.BlockSpec(memory_space=pltpu.VMEM)],
        out_specs=(pl.BlockSpec(memory_space=pltpu.VMEM),) * 2,
        compiler_params=pltpu.CompilerParams(vmem_limit_bytes=1 << 20),
        name="factor",
    )(g)


def basis_kernel(linv_ref, *refs):
    y_refs, out_ref, table = refs[:-2], refs[-2], refs[-1]
    cols, parts, _, nvar = out_ref.shape[:4]
    count = linv_ref.shape[0]
    af = lax.axis_index("af")
    for c in range(cols):
        line = linv_ref[pl.ds(af * cols + c, 1), :]
        for u in range(count):
            table[c * count + u] = jnp.broadcast_to(line[:, u : u + 1], (SUB, LANE))
    for k, y_ref in enumerate(y_refs):
        plane = lax.bitwise_xor(af, k)
        for part in range(parts):
            sums = [[None] * nvar for _ in range(cols)]
            for u in range(count):
                values = [y_ref[u, part * nvar + v] for v in range(nvar)]
                for c in range(cols):
                    times = table[c * count + u]
                    for v in range(nvar):
                        term = times * values[v]
                        sums[c][v] = term if u == 0 else sums[c][v] + term
            for c in range(cols):
                for v in range(nvar):
                    out_ref[c, part, plane, v, :, :LANE] = sums[c][v][: SUB // 2]
                    out_ref[c, part, plane, v, :, LANE:] = sums[c][v][SUB // 2 :]


def basis_of(linv, ys, shape):
    return pl.pallas_call(
        basis_kernel,
        out_shape=jax.ShapeDtypeStruct(shape, jnp.float32),
        in_specs=[pl.BlockSpec(memory_space=pltpu.VMEM)] * (1 + len(ys)),
        out_specs=pl.BlockSpec(memory_space=pltpu.VMEM),
        scratch_shapes=[pltpu.VMEM((shape[0] * linv.shape[0], SUB, LANE), jnp.float32)],
        compiler_params=pltpu.CompilerParams(vmem_limit_bytes=8 << 20),
        name="basis",
    )(linv, *ys)


def on_device(size_x, size_f, forcing, flow, sponge, coupling, omega):
    cols, parts, planes, nvar, rad, azi = forcing.shape
    groups = size_x // cols
    two_sided = groups != 2
    assert rad * azi == SUB * LANE and azi == 2 * LANE and size_x % cols == 0
    assert planes == size_f and 2 * planes == SWEEPS and cols == 4
    dims = (cols, parts, planes, nvar, groups)

    slabs = pack(forcing, sponge, flow)
    halo = []
    for k in range(cols):
        pairs = []
        for g in range(size_x):
            group, j = divmod(g, cols)
            target = group - 1 if j < cols // 2 else group + 1
            if 0 <= target < groups:
                pairs.append((g, target * cols + (j ^ k)))
        halo.append(lax.ppermute(slabs[k], "gx", pairs))
    mine = [slabs[0]]
    for k in range(1, cols):
        pairs = [(g, g ^ k) for g in range(size_x)]
        mine.append(lax.ppermute(slabs[k], "gx", pairs))
    state = sweeps(coupling, omega, mine, dims, two_sided)
    z = sweeps(coupling, omega, halo, dims, two_sided, state)[0]

    together = [
        [(q * cols + j) * size_f + a for a in range(size_f) for j in range(cols)] for q in range(groups)
    ]
    y = lax.all_to_all(z, ("gx", "af"), 0, 0, axis_index_groups=together, tiled=True)
    ys = [y] + [None] * (size_f - 1)
    ys[2] = lax.ppermute(y, "af", [(a, a ^ 2) for a in range(size_f)])
    ys[1] = lax.ppermute(y, "af", [(a, a ^ 1) for a in range(size_f)])
    g = gram(y)
    step = 1
    while step < size_x:
        far = min(4, size_x // step) if step > 1 else 2
        others = [
            lax.ppermute(g, "gx", [(x, x ^ (step * k)) for x in range(size_x)]) for k in range(1, far)
        ]
        for other in others:
            g = g + other
        step *= far
    for k in (1, 2):
        g = g + lax.ppermute(g, "af", [(x, x ^ k) for x in range(size_f)])
    g, ys[2] = lax.optimization_barrier((g, ys[2]))
    ys[3] = lax.ppermute(ys[2], "af", [(x, x ^ 1) for x in range(size_f)])
    length = parts * planes * nvar * rad * azi * size_x
    coeff, linv = factor(g, length)
    return basis_of(linv, ys, forcing.shape), coeff


def solution(mesh):
    placed = (
        P("af", None, "gx", None, None, None),
        P("gx", None, None),
        P("gx", None, None),
        P(),
        P(),
    )

    def body(*args):
        return on_device(mesh.shape["gx"], mesh.shape["af"], *args)

    return jax.shard_map(
        body,
        mesh=mesh,
        in_specs=placed,
        out_specs=(P("af", None, "gx", None, None, None), P()),
        check_vma=False,
    )
```

```python
import functools

import jax
import jax.numpy as jnp
from jax import lax
from jax.experimental import pallas as pl
from jax.experimental.pallas import tpu as pltpu
from jax.sharding import PartitionSpec as P


FORCINGS = 8
SWEEPS = 8

viscosity = 0.25
SUB, LANE = 8, 128
EXACT = lax.Precision.HIGHEST


def fold(plane):
    return jnp.concatenate([plane[:, :LANE], plane[:, LANE:]], axis=0)


def pack_kernel(forcing_hbm, sponge_hbm, flow_hbm, *refs):
    cols, parts, planes, nvar = forcing_hbm.shape[:4]
    out_refs, (forcing_ref, sponge_ref, flow_ref, sems) = refs[:cols], refs[cols:]
    me = lax.rem(lax.axis_index("gx"), cols)
    rows = parts * planes * nvar
    copies = []
    for k in range(cols):
        col = lax.bitwise_xor(me, k)
        copies.append(pltpu.make_async_copy(forcing_hbm.at[col], forcing_ref.at[k], sems.at[k]))
    copies.append(pltpu.make_async_copy(sponge_hbm, sponge_ref, sems.at[cols]))
    copies.append(pltpu.make_async_copy(flow_hbm, flow_ref, sems.at[cols + 1]))
    for copy in copies:
        copy.start()
    for copy in copies[cols:]:
        copy.wait()
    for plane in range(planes):
        sponge, flow = fold(sponge_ref[plane]), fold(flow_ref[plane])
        for out_ref in out_refs:
            out_ref[rows + plane] = sponge
            out_ref[rows + planes + plane] = flow
    for k, out_ref in enumerate(out_refs):
        copies[k].wait()
        for part in range(parts):
            for plane in range(planes):
                for v in range(nvar):
                    row = (part * planes + plane) * nvar + v
                    out_ref[row] = fold(forcing_ref[k, part, plane, v])


def in_place(*arrays):
    return tuple(pltpu.with_memory_space_constraint(a, pltpu.HBM) for a in arrays)


def pack(forcing, sponge, flow):
    cols, parts, planes, nvar = forcing.shape[:4]
    rows = planes * (parts * nvar + 2)
    slab = jax.ShapeDtypeStruct((rows, SUB, LANE), jnp.float32)
    return pl.pallas_call(
        pack_kernel,
        out_shape=(slab,) * cols,
        in_specs=[pl.BlockSpec(memory_space=pltpu.HBM)] * 3,
        out_specs=(pl.BlockSpec(memory_space=pltpu.VMEM),) * cols,
        scratch_shapes=[
            pltpu.VMEM(forcing.shape, jnp.float32),
            pltpu.VMEM(sponge.shape, jnp.float32),
            pltpu.VMEM(flow.shape, jnp.float32),
            pltpu.SemaphoreType.DMA((cols + 2,)),
        ],
        compiler_params=pltpu.CompilerParams(vmem_limit_bytes=4 << 20),
        name="pack",
    )(*in_place(forcing, sponge, flow))


def sweep_kernel(dims, two_sided, outer, *refs):
    cols, parts, planes, nvar, groups = dims
    comp = parts * nvar
    state = 8
    coupling_hbm, omega_hbm = refs[:2]
    slab_refs = refs[2 : 2 + cols]
    at = 2 + cols + (state if outer else 0)
    out_ref, first, even, odd, p_re, p_im, w_lo, w_hi = refs[at : at + state]
    raw, coupling_ref, omega_ref, sems = refs[at + state :]
    gx = lax.axis_index("gx")
    me, group = lax.rem(gx, cols), lax.div(gx, cols)
    flip = jnp.int32(0) if two_sided else jnp.int32(group)
    rows = planes * (comp + 2)
    own, span = cols * planes, SWEEPS
    begin = span if two_sided else 0
    end = begin + own
    window = end + span

    scalars = [
        pltpu.make_async_copy(coupling_hbm, coupling_ref, sems.at[cols]),
        pltpu.make_async_copy(omega_hbm, omega_ref, sems.at[cols + 1]),
    ]
    for copy in scalars:
        copy.start()
    copies = []
    for k, slab_ref in enumerate(slab_refs):
        slot = lax.bitwise_xor(me, k)
        copies.append(pltpu.make_async_copy(slab_ref, raw.at[pl.ds(slot * rows, rows)], sems.at[k]))
        copies[-1].start()

    for copy in scalars:
        copy.wait()
    column = lax.axis_index("af") * cols + me
    freq = jnp.where(column < FORCINGS, omega_ref[0], omega_ref[1])
    side = jnp.where(flip == 1, -2.0, 2.0).astype(jnp.float32)
    if not outer:
        for ref in (first, even, odd):
            for c in range(comp):
                ref[c] = jnp.zeros((SUB, LANE), jnp.float32)
    for copy in copies:
        copy.wait()

    def prepare(i, _):
        slab, inner = lax.div(i - begin + span, planes) - span // planes, lax.rem(i, planes)
        if two_sided:
            slot = jnp.where(slab < 0, slab + cols, lax.rem(slab, cols))
            inside = jnp.logical_and(
                jnp.logical_or(i >= begin, group > 0), jnp.logical_or(i < end, group < groups - 1)
            )
            keep = jnp.where(inside, 1.0, 0.0).astype(jnp.float32)
        else:
            slot = lax.rem(slab, cols)
            slot = jnp.where(flip == 1, cols - 1 - slot, slot)
            inner = jnp.where(flip == 1, planes - 1 - inner, inner)
        base = slot * rows
        sponge = raw[base + planes * comp + inner]
        flow = raw[base + planes * comp + planes + inner]
        w_lo[i] = 1.0 - side * flow
        w_hi[i] = 1.0 + side * flow
        for v in range(nvar):
            diag = sponge + (6.0 * viscosity - coupling_ref[v, v])
            scale = 1.0 / (diag * diag + freq * freq)
            if two_sided:
                scale = scale * keep
            pr, pi = diag * scale, freq * scale
            f_re = raw[base + inner * nvar + v]
            f_im = raw[base + planes * nvar + inner * nvar + v]
            first[(i + 1) * comp + v] = pr * f_re - pi * f_im
            first[(i + 1) * comp + nvar + v] = pr * f_im + pi * f_re
            p_re[i * nvar + v] = viscosity * pr
            p_im[i * nvar + v] = viscosity * pi
        return 0

    if outer:
        lax.fori_loop(end, window, prepare, 0)
        if two_sided:
            lax.fori_loop(0, begin, prepare, 0)
    else:
        lax.fori_loop(begin, end, prepare, 0)

    lane = lax.broadcasted_iota(jnp.int32, (SUB, LANE), 1)
    radial = lax.rem(lax.broadcasted_iota(jnp.int32, (SUB, LANE), 0), SUB // 2)
    at_last, at_first = lane == LANE - 1, lane == 0
    at_outer, at_axis = radial == SUB // 2 - 1, radial == 0
    pull = [[coupling_ref[u, v] * (1.0 / viscosity) for v in range(nvar)] for u in range(nvar)]

    def update(i, src, emit):
        field = [src[(i + 1) * comp + c] for c in range(comp)]
        lo, hi = w_lo[i], w_hi[i]
        for v in range(nvar):
            sums = []
            for part in range(parts):
                c = part * nvar + v
                z = field[c]
                other = pltpu.roll(z, SUB // 2, 0)
                total = pltpu.roll(jnp.where(at_last, other, z), 1, 1)
                total = total + pltpu.roll(jnp.where(at_first, other, z), LANE - 1, 1)
                total = total + jnp.where(at_axis, 0.0, pltpu.roll(z, 1, 0))
                total = total + jnp.where(at_outer, 0.0, pltpu.roll(z, SUB - 1, 0))
                total = total + lo * src[i * comp + c]
                total = total + hi * src[(i + 2) * comp + c]
                for u in range(nvar):
                    if u != v:
                        total = total + pull[u][v] * field[part * nvar + u]
                sums.append(total)
            pr, pi = p_re[i * nvar + v], p_im[i * nvar + v]
            emit(i, v, first[(i + 1) * comp + v] + (pr * sums[0] - pi * sums[1]))
            emit(i, nvar + v, first[(i + 1) * comp + nvar + v] + (pr * sums[1] + pi * sums[0]))

    def level(src, emit, lo, hi, unroll=2):
        def body(n, _):
            for m in range(unroll):
                update(lo + n * unroll + m, src, emit)
            return 0

        trips = (hi - lo) // unroll
        lax.fori_loop(0, trips, body, 0)
        for i in range(lo + trips * unroll, hi):
            update(jnp.int32(i), src, emit)

    def into(ref):
        def emit(i, c, value):
            ref[(i + 1) * comp + c] = value

        return emit

    def finish(i, c, value):
        plane = i - begin if two_sided else jnp.where(flip == 1, own - 1 - i, i)
        out_ref[lax.rem(plane, planes) * cols + lax.div(plane, planes), c] = value

    src = first
    for s in range(1, SWEEPS + 1):
        dst = odd if s % 2 else even
        emit = finish if s == SWEEPS else into(dst)
        if outer:
            if two_sided:
                level(src, emit, s, begin + s)
            level(src, emit, end - s, window - s)
        else:
            level(src, emit, begin + s if two_sided else 0, end - s)
        src = dst


def sweeps(coupling, omega, slabs, dims, two_sided, state=()):
    cols, parts, planes, nvar, _ = dims
    comp = parts * nvar
    own = cols * planes
    window = own + SWEEPS * (2 if two_sided else 1)
    tiles = lambda n: jax.ShapeDtypeStruct((n, SUB, LANE), jnp.float32)
    shapes = [jax.ShapeDtypeStruct((own, comp, SUB, LANE), jnp.float32)]
    shapes += [tiles((window + 2) * comp)] * 3 + [tiles(window * nvar)] * 2 + [tiles(window)] * 2
    fast = pl.BlockSpec(memory_space=pltpu.VMEM)
    lead = 2 + len(slabs)
    return pl.pallas_call(
        functools.partial(sweep_kernel, dims, two_sided, bool(state)),
        out_shape=shapes,
        in_specs=[pl.BlockSpec(memory_space=pltpu.HBM)] * 2
        + [pl.BlockSpec(memory_space=pl.ANY)] * len(slabs)
        + [fast] * len(state),
        out_specs=[fast] * len(shapes),
        scratch_shapes=[
            pltpu.VMEM((cols * planes * (comp + 2), SUB, LANE), jnp.float32),
            pltpu.SMEM(coupling.shape, jnp.float32),
            pltpu.SMEM(omega.shape, jnp.float32),
            pltpu.SemaphoreType.DMA((cols + 2,)),
        ],
        input_output_aliases={lead + n: n for n in range(len(state))},
        compiler_params=pltpu.CompilerParams(vmem_limit_bytes=16 << 20),
        cost_estimate=pl.CostEstimate(flops=6_000_000_000, bytes_accessed=1 << 20, transcendentals=0),
        name="outer" if state else "inner",
    )(*in_place(coupling, omega), *slabs, *state)


def gram_kernel(y_ref, g_ref):
    count, comp = y_ref.shape[:2]
    rows = count * SUB
    pair = (((1,), (1,)), ((), ()))

    def times(a, b):
        return lax.dot_general(a, b, pair, preferred_element_type=jnp.float32)

    even = jnp.zeros((rows, rows), jnp.float32)
    mixed = jnp.zeros((rows, rows), jnp.float32)
    for c in range(0, comp, 2):
        x = jnp.concatenate([y_ref[:, c].reshape(rows, LANE), y_ref[:, c + 1].reshape(rows, LANE)], axis=1)
        high = x.astype(jnp.bfloat16)
        rest = x - high.astype(jnp.float32)
        mid = rest.astype(jnp.bfloat16)
        low = (rest - mid.astype(jnp.float32)).astype(jnp.bfloat16)
        even = even + times(high, high) + times(mid, mid)
        mixed = mixed + times(high, mid) + times(high, low)
    row = lax.broadcasted_iota(jnp.int32, (rows, rows), 0)
    col = lax.broadcasted_iota(jnp.int32, (rows, rows), 1)
    same = lax.rem(row, SUB) == lax.rem(col, SUB)

    def gather(total):
        return jnp.sum(jnp.where(same, total, 0.0).reshape(count, SUB, rows), axis=1)

    owner = lax.div(lax.broadcasted_iota(jnp.int32, (count, rows), 1), SUB)
    member = (owner == lax.broadcasted_iota(jnp.int32, (count, rows), 0)).astype(jnp.float32)
    one = gather(mixed)
    both = gather(even) + one
    exact = functools.partial(lax.dot_general, precision=EXACT, preferred_element_type=jnp.float32)
    g = exact(both, member, pair) + exact(member, one, pair)
    g = jnp.concatenate([g, jnp.zeros((count, LANE - count), jnp.float32)], axis=1)
    for x in range(g_ref.shape[0]):
        g_ref[x] = g


def gram(y, copies):
    count = y.shape[0]
    return pl.pallas_call(
        gram_kernel,
        out_shape=jax.ShapeDtypeStruct((copies, count, LANE), jnp.float32),
        in_specs=[pl.BlockSpec(memory_space=pltpu.VMEM)],
        out_specs=pl.BlockSpec(memory_space=pltpu.VMEM),
        compiler_params=pltpu.CompilerParams(vmem_limit_bytes=4 << 20),
        cost_estimate=pl.CostEstimate(flops=2_000_000_000, bytes_accessed=1 << 20, transcendentals=0),
        name="gram",
    )(y)


def add_kernel(parts_ref, out_ref):
    total = parts_ref[0]
    for x in range(1, parts_ref.shape[0]):
        total = total + parts_ref[x]
    out_ref[...] = total


def add_up(parts):
    return pl.pallas_call(
        add_kernel,
        out_shape=jax.ShapeDtypeStruct(parts.shape[1:], jnp.float32),
        in_specs=[pl.BlockSpec(memory_space=pltpu.VMEM)],
        out_specs=pl.BlockSpec(memory_space=pltpu.VMEM),
        compiler_params=pltpu.CompilerParams(vmem_limit_bytes=2 << 20),
        name="add",
    )(parts)


def factor_kernel(length, near_ref, far_ref, coeff_ref, linv_ref):
    n = coeff_ref.shape[0]
    row = lax.broadcasted_iota(jnp.int32, (n, n), 0)
    col = lax.broadcasted_iota(jnp.int32, (n, n), 1)
    left = (near_ref[...] + far_ref[...])[:, :n]
    right = (row == col).astype(jnp.float32)
    upper, lower = jnp.zeros((n, n), jnp.float32), jnp.zeros((n, n), jnp.float32)
    for k in range(n):
        pivot = left[k : k + 1, k : k + 1]
        left_row, right_row = left[k : k + 1, :], right[k : k + 1, :]
        root = 1.0 / jnp.sqrt(pivot)
        upper = jnp.where(row == k, left_row * root, upper)
        lower = jnp.where(row == k, right_row * root, lower)
        times = jnp.where(row > k, left[:, k : k + 1] / pivot, 0.0)
        left = left - times * left_row
        right = right - times * right_row
    coeff_ref[...] = jnp.where(col >= row, upper, 0.0) / jnp.sqrt(jnp.float32(length))
    linv_ref[...] = lower * jnp.sqrt(jnp.float32(length))


def factor(near, far, length):
    square = jax.ShapeDtypeStruct((near.shape[0],) * 2, jnp.float32)
    return pl.pallas_call(
        functools.partial(factor_kernel, length),
        out_shape=(square, square),
        in_specs=[pl.BlockSpec(memory_space=pltpu.VMEM)] * 2,
        out_specs=(pl.BlockSpec(memory_space=pltpu.VMEM),) * 2,
        compiler_params=pltpu.CompilerParams(vmem_limit_bytes=1 << 20),
        name="factor",
    )(near, far)


def basis_kernel(linv_ref, *refs):
    y_refs, out_ref, table = refs[:-2], refs[-2], refs[-1]
    cols, parts, _, nvar = out_ref.shape[:4]
    count = linv_ref.shape[0]
    af = lax.axis_index("af")
    for c in range(cols):
        line = linv_ref[pl.ds(af * cols + c, 1), :]
        for u in range(count):
            table[c * count + u] = jnp.broadcast_to(line[:, u : u + 1], (SUB, LANE))
    for k, y_ref in enumerate(y_refs):
        plane = lax.bitwise_xor(af, k)
        for part in range(parts):
            sums = [[None] * nvar for _ in range(cols)]
            for u in range(count):
                values = [y_ref[u, part * nvar + v] for v in range(nvar)]
                for c in range(cols):
                    times = table[c * count + u]
                    for v in range(nvar):
                        term = times * values[v]
                        sums[c][v] = term if u == 0 else sums[c][v] + term
            for c in range(cols):
                for v in range(nvar):
                    out_ref[c, part, plane, v, :, :LANE] = sums[c][v][: SUB // 2]
                    out_ref[c, part, plane, v, :, LANE:] = sums[c][v][SUB // 2 :]


def basis_of(linv, ys, shape):
    return pl.pallas_call(
        basis_kernel,
        out_shape=jax.ShapeDtypeStruct(shape, jnp.float32),
        in_specs=[pl.BlockSpec(memory_space=pltpu.VMEM)] * (1 + len(ys)),
        out_specs=pl.BlockSpec(memory_space=pltpu.VMEM),
        scratch_shapes=[pltpu.VMEM((shape[0] * linv.shape[0], SUB, LANE), jnp.float32)],
        compiler_params=pltpu.CompilerParams(vmem_limit_bytes=8 << 20),
        name="basis",
    )(linv, *ys)


def on_device(size_x, size_f, forcing, flow, sponge, coupling, omega):
    cols, parts, planes, nvar, rad, azi = forcing.shape
    groups = size_x // cols
    two_sided = groups != 2
    assert rad * azi == SUB * LANE and azi == 2 * LANE and size_x % cols == 0
    assert planes == size_f and 2 * planes == SWEEPS and cols == 4
    dims = (cols, parts, planes, nvar, groups)

    slabs = pack(forcing, sponge, flow)
    halo = []
    for k in range(cols):
        pairs = []
        for g in range(size_x):
            group, j = divmod(g, cols)
            target = group - 1 if j < cols // 2 else group + 1
            if 0 <= target < groups:
                pairs.append((g, target * cols + (j ^ k)))
        halo.append(lax.ppermute(slabs[k], "gx", pairs))
    mine = [slabs[0]]
    for k in range(1, cols):
        pairs = [(g, g ^ k) for g in range(size_x)]
        mine.append(lax.ppermute(slabs[k], "gx", pairs))
    state = sweeps(coupling, omega, mine, dims, two_sided)
    z = sweeps(coupling, omega, halo, dims, two_sided, state)[0]

    together = [
        [(q * cols + j) * size_f + a for a in range(size_f) for j in range(cols)] for q in range(groups)
    ]
    y = lax.all_to_all(z, ("gx", "af"), 0, 0, axis_index_groups=together, tiled=True)
    ys = [y] + [None] * (size_f - 1)
    ys[2] = lax.ppermute(y, "af", [(a, a ^ 2) for a in range(size_f)])
    ys[1] = lax.ppermute(y, "af", [(a, a ^ 1) for a in range(size_f)])
    g = add_up(lax.all_to_all(gram(y, size_x), "gx", 0, 0, tiled=True))
    g = g + lax.ppermute(g, "af", [(x, x ^ 1) for x in range(size_f)])
    far = lax.ppermute(g, "af", [(x, x ^ 2) for x in range(size_f)])
    far, ys[2] = lax.optimization_barrier((far, ys[2]))
    ys[3] = lax.ppermute(ys[2], "af", [(x, x ^ 1) for x in range(size_f)])
    length = parts * planes * nvar * rad * azi * size_x
    coeff, linv = factor(g, far, length)
    return basis_of(linv, ys, forcing.shape), coeff


def solution(mesh):
    placed = (
        P("af", None, "gx", None, None, None),
        P("gx", None, None),
        P("gx", None, None),
        P(),
        P(),
    )

    def body(*args):
        return on_device(mesh.shape["gx"], mesh.shape["af"], *args)

    return jax.shard_map(
        body,
        mesh=mesh,
        in_specs=placed,
        out_specs=(P("af", None, "gx", None, None, None), P()),
        check_vma=False,
    )
```

```python
import functools

import jax
import jax.numpy as jnp
from jax import lax
from jax.experimental import pallas as pl
from jax.experimental.pallas import tpu as pltpu
from jax.sharding import PartitionSpec as P


FORCINGS = 8
SWEEPS = 8

viscosity = 0.25
SUB, LANE = 8, 128
EXACT = lax.Precision.HIGHEST


def fold(plane):
    return jnp.concatenate([plane[:, :LANE], plane[:, LANE:]], axis=0)


def pack_kernel(forcing_hbm, sponge_hbm, flow_hbm, *refs):
    cols, parts, planes, nvar = forcing_hbm.shape[:4]
    out_refs, (forcing_ref, sponge_ref, flow_ref, sems) = refs[:cols], refs[cols:]
    me = lax.rem(lax.axis_index("gx"), cols)
    rows = parts * planes * nvar
    copies = []
    for k in range(cols):
        col = lax.bitwise_xor(me, k)
        copies.append(pltpu.make_async_copy(forcing_hbm.at[col], forcing_ref.at[k], sems.at[k]))
    copies.append(pltpu.make_async_copy(sponge_hbm, sponge_ref, sems.at[cols]))
    copies.append(pltpu.make_async_copy(flow_hbm, flow_ref, sems.at[cols + 1]))
    for copy in copies:
        copy.start()
    for copy in copies[cols:]:
        copy.wait()
    for plane in range(planes):
        sponge, flow = fold(sponge_ref[plane]), fold(flow_ref[plane])
        for out_ref in out_refs:
            out_ref[rows + plane] = sponge
            out_ref[rows + planes + plane] = flow
    for k, out_ref in enumerate(out_refs):
        copies[k].wait()
        for part in range(parts):
            for plane in range(planes):
                for v in range(nvar):
                    row = (part * planes + plane) * nvar + v
                    out_ref[row] = fold(forcing_ref[k, part, plane, v])


def in_place(*arrays):
    return tuple(pltpu.with_memory_space_constraint(a, pltpu.HBM) for a in arrays)


def pack(forcing, sponge, flow):
    cols, parts, planes, nvar = forcing.shape[:4]
    rows = planes * (parts * nvar + 2)
    slab = jax.ShapeDtypeStruct((rows, SUB, LANE), jnp.float32)
    return pl.pallas_call(
        pack_kernel,
        out_shape=(slab,) * cols,
        in_specs=[pl.BlockSpec(memory_space=pltpu.HBM)] * 3,
        out_specs=(pl.BlockSpec(memory_space=pltpu.VMEM),) * cols,
        scratch_shapes=[
            pltpu.VMEM(forcing.shape, jnp.float32),
            pltpu.VMEM(sponge.shape, jnp.float32),
            pltpu.VMEM(flow.shape, jnp.float32),
            pltpu.SemaphoreType.DMA((cols + 2,)),
        ],
        compiler_params=pltpu.CompilerParams(vmem_limit_bytes=4 << 20),
        name="pack",
    )(*in_place(forcing, sponge, flow))


def sweep_kernel(dims, two_sided, outer, *refs):
    cols, parts, planes, nvar, groups = dims
    comp = parts * nvar
    state = 8
    coupling_hbm, omega_hbm = refs[:2]
    slab_refs = refs[2 : 2 + cols]
    at = 2 + cols + (state if outer else 0)
    out_ref, first, even, odd, p_re, p_im, w_lo, w_hi = refs[at : at + state]
    raw, coupling_ref, omega_ref, sems = refs[at + state :]
    gx = lax.axis_index("gx")
    me, group = lax.rem(gx, cols), lax.div(gx, cols)
    flip = jnp.int32(0) if two_sided else jnp.int32(group)
    rows = planes * (comp + 2)
    own, span = cols * planes, SWEEPS
    begin = span if two_sided else 0
    end = begin + own
    window = end + span

    scalars = [
        pltpu.make_async_copy(coupling_hbm, coupling_ref, sems.at[cols]),
        pltpu.make_async_copy(omega_hbm, omega_ref, sems.at[cols + 1]),
    ]
    for copy in scalars:
        copy.start()
    copies = []
    for k, slab_ref in enumerate(slab_refs):
        slot = lax.bitwise_xor(me, k)
        copies.append(pltpu.make_async_copy(slab_ref, raw.at[pl.ds(slot * rows, rows)], sems.at[k]))
        copies[-1].start()

    for copy in scalars:
        copy.wait()
    column = lax.axis_index("af") * cols + me
    freq = jnp.where(column < FORCINGS, omega_ref[0], omega_ref[1])
    side = jnp.where(flip == 1, -2.0, 2.0).astype(jnp.float32)
    if not outer:
        for ref in (first, even, odd):
            for c in range(comp):
                ref[c] = jnp.zeros((SUB, LANE), jnp.float32)
    for copy in copies:
        copy.wait()

    def prepare(i, _):
        slab, inner = lax.div(i - begin + span, planes) - span // planes, lax.rem(i, planes)
        if two_sided:
            slot = jnp.where(slab < 0, slab + cols, lax.rem(slab, cols))
            inside = jnp.logical_and(
                jnp.logical_or(i >= begin, group > 0), jnp.logical_or(i < end, group < groups - 1)
            )
            keep = jnp.where(inside, 1.0, 0.0).astype(jnp.float32)
        else:
            slot = lax.rem(slab, cols)
            slot = jnp.where(flip == 1, cols - 1 - slot, slot)
            inner = jnp.where(flip == 1, planes - 1 - inner, inner)
        base = slot * rows
        sponge = raw[base + planes * comp + inner]
        flow = raw[base + planes * comp + planes + inner]
        w_lo[i] = 1.0 - side * flow
        w_hi[i] = 1.0 + side * flow
        for v in range(nvar):
            diag = sponge + (6.0 * viscosity - coupling_ref[v, v])
            scale = 1.0 / (diag * diag + freq * freq)
            if two_sided:
                scale = scale * keep
            pr, pi = diag * scale, freq * scale
            f_re = raw[base + inner * nvar + v]
            f_im = raw[base + planes * nvar + inner * nvar + v]
            first[(i + 1) * comp + v] = pr * f_re - pi * f_im
            first[(i + 1) * comp + nvar + v] = pr * f_im + pi * f_re
            p_re[i * nvar + v] = viscosity * pr
            p_im[i * nvar + v] = viscosity * pi
        return 0

    if outer:
        lax.fori_loop(end, window, prepare, 0)
        if two_sided:
            lax.fori_loop(0, begin, prepare, 0)
    else:
        lax.fori_loop(begin, end, prepare, 0)

    lane = lax.broadcasted_iota(jnp.int32, (SUB, LANE), 1)
    radial = lax.rem(lax.broadcasted_iota(jnp.int32, (SUB, LANE), 0), SUB // 2)
    at_last, at_first = lane == LANE - 1, lane == 0
    at_outer, at_axis = radial == SUB // 2 - 1, radial == 0
    pull = [[coupling_ref[u, v] * (1.0 / viscosity) for v in range(nvar)] for u in range(nvar)]

    def update(i, src, emit):
        field = [src[(i + 1) * comp + c] for c in range(comp)]
        lo, hi = w_lo[i], w_hi[i]
        lines = src.reshape(src.shape[0] * SUB, LANE)
        start = (i + 1) * comp * SUB
        for v in range(nvar):
            sums = []
            for part in range(parts):
                c = part * nvar + v
                z = field[c]
                other = pltpu.roll(z, SUB // 2, 0)
                left = pltpu.roll(jnp.where(at_last, other, z), 1, 1)
                right = pltpu.roll(jnp.where(at_first, other, z), LANE - 1, 1)
                down = jnp.where(at_axis, 0.0, lines[pl.ds(start + c * SUB - 1, SUB), :])
                up = jnp.where(at_outer, 0.0, lines[pl.ds(start + c * SUB + 1, SUB), :])
                total = (lo * src[i * comp + c] + hi * src[(i + 2) * comp + c]) + (down + up)
                for u in range(nvar):
                    if u != v:
                        total = total + pull[u][v] * field[part * nvar + u]
                sums.append(total + (left + right))
            pr, pi = p_re[i * nvar + v], p_im[i * nvar + v]
            emit(i, v, first[(i + 1) * comp + v] + (pr * sums[0] - pi * sums[1]))
            emit(i, nvar + v, first[(i + 1) * comp + nvar + v] + (pr * sums[1] + pi * sums[0]))

    def level(src, emit, lo, hi, unroll=8):
        def body(n, _):
            for m in range(unroll):
                update(lo + n * unroll + m, src, emit)
            return 0

        trips = (hi - lo) // unroll
        lax.fori_loop(0, trips, body, 0)
        for i in range(lo + trips * unroll, hi):
            update(jnp.int32(i), src, emit)

    def into(ref):
        def emit(i, c, value):
            ref[(i + 1) * comp + c] = value

        return emit

    def finish(i, c, value):
        plane = i - begin if two_sided else jnp.where(flip == 1, own - 1 - i, i)
        out_ref[lax.rem(plane, planes) * cols + lax.div(plane, planes), c] = value

    src = first
    for s in range(1, SWEEPS + 1):
        dst = odd if s % 2 else even
        emit = finish if s == SWEEPS else into(dst)
        if outer:
            if two_sided:
                level(src, emit, s, begin + s)
            level(src, emit, end - s, window - s)
        else:
            level(src, emit, begin + s if two_sided else 0, end - s)
        src = dst


def sweeps(coupling, omega, slabs, dims, two_sided, state=()):
    cols, parts, planes, nvar, _ = dims
    comp = parts * nvar
    own = cols * planes
    window = own + SWEEPS * (2 if two_sided else 1)
    tiles = lambda n: jax.ShapeDtypeStruct((n, SUB, LANE), jnp.float32)
    shapes = [jax.ShapeDtypeStruct((own, comp, SUB, LANE), jnp.float32)]
    shapes += [tiles((window + 2) * comp)] * 3 + [tiles(window * nvar)] * 2 + [tiles(window)] * 2
    fast = pl.BlockSpec(memory_space=pltpu.VMEM)
    lead = 2 + len(slabs)
    return pl.pallas_call(
        functools.partial(sweep_kernel, dims, two_sided, bool(state)),
        out_shape=shapes,
        in_specs=[pl.BlockSpec(memory_space=pltpu.HBM)] * 2
        + [pl.BlockSpec(memory_space=pl.ANY)] * len(slabs)
        + [fast] * len(state),
        out_specs=[fast] * len(shapes),
        scratch_shapes=[
            pltpu.VMEM((cols * planes * (comp + 2), SUB, LANE), jnp.float32),
            pltpu.SMEM(coupling.shape, jnp.float32),
            pltpu.SMEM(omega.shape, jnp.float32),
            pltpu.SemaphoreType.DMA((cols + 2,)),
        ],
        input_output_aliases={lead + n: n for n in range(len(state))},
        compiler_params=pltpu.CompilerParams(vmem_limit_bytes=16 << 20),
        cost_estimate=pl.CostEstimate(flops=6_000_000_000, bytes_accessed=1 << 20, transcendentals=0),
        name="outer" if state else "inner",
    )(*in_place(coupling, omega), *slabs, *state)


def gram_kernel(y_ref, g_ref):
    count, comp = y_ref.shape[:2]
    rows = count * SUB
    pair = (((1,), (1,)), ((), ()))

    def times(a, b):
        return lax.dot_general(a, b, pair, preferred_element_type=jnp.float32)

    even = jnp.zeros((rows, rows), jnp.float32)
    mixed = jnp.zeros((rows, rows), jnp.float32)
    for c in range(0, comp, 2):
        x = jnp.concatenate([y_ref[:, c].reshape(rows, LANE), y_ref[:, c + 1].reshape(rows, LANE)], axis=1)
        high = x.astype(jnp.bfloat16)
        rest = x - high.astype(jnp.float32)
        mid = rest.astype(jnp.bfloat16)
        low = (rest - mid.astype(jnp.float32)).astype(jnp.bfloat16)
        even = even + times(high, high) + times(mid, mid)
        mixed = mixed + times(high, mid) + times(high, low)
    row = lax.broadcasted_iota(jnp.int32, (rows, rows), 0)
    col = lax.broadcasted_iota(jnp.int32, (rows, rows), 1)
    same = lax.rem(row, SUB) == lax.rem(col, SUB)

    def gather(total):
        return jnp.sum(jnp.where(same, total, 0.0).reshape(count, SUB, rows), axis=1)

    owner = lax.div(lax.broadcasted_iota(jnp.int32, (count, rows), 1), SUB)
    member = (owner == lax.broadcasted_iota(jnp.int32, (count, rows), 0)).astype(jnp.float32)
    one = gather(mixed)
    both = gather(even) + one
    exact = functools.partial(lax.dot_general, precision=EXACT, preferred_element_type=jnp.float32)
    g = exact(both, member, pair) + exact(member, one, pair)
    g = jnp.concatenate([g, jnp.zeros((count, LANE - count), jnp.float32)], axis=1)
    for x in range(g_ref.shape[0]):
        g_ref[x] = g


def gram(y, copies):
    count = y.shape[0]
    return pl.pallas_call(
        gram_kernel,
        out_shape=jax.ShapeDtypeStruct((copies, count, LANE), jnp.float32),
        in_specs=[pl.BlockSpec(memory_space=pltpu.VMEM)],
        out_specs=pl.BlockSpec(memory_space=pltpu.VMEM),
        compiler_params=pltpu.CompilerParams(vmem_limit_bytes=4 << 20),
        cost_estimate=pl.CostEstimate(flops=2_000_000_000, bytes_accessed=1 << 20, transcendentals=0),
        name="gram",
    )(y)


def add_kernel(parts_ref, out_ref):
    total = parts_ref[0]
    for x in range(1, parts_ref.shape[0]):
        total = total + parts_ref[x]
    out_ref[...] = total


def add_up(parts):
    return pl.pallas_call(
        add_kernel,
        out_shape=jax.ShapeDtypeStruct(parts.shape[1:], jnp.float32),
        in_specs=[pl.BlockSpec(memory_space=pltpu.VMEM)],
        out_specs=pl.BlockSpec(memory_space=pltpu.VMEM),
        compiler_params=pltpu.CompilerParams(vmem_limit_bytes=2 << 20),
        name="add",
    )(parts)


def factor_kernel(length, near_ref, far_ref, coeff_ref, linv_ref):
    n = coeff_ref.shape[0]
    row = lax.broadcasted_iota(jnp.int32, (n, n), 0)
    col = lax.broadcasted_iota(jnp.int32, (n, n), 1)
    left = (near_ref[...] + far_ref[...])[:, :n]
    right = (row == col).astype(jnp.float32)
    upper, lower = jnp.zeros((n, n), jnp.float32), jnp.zeros((n, n), jnp.float32)
    for k in range(n):
        pivot = left[k : k + 1, k : k + 1]
        left_row, right_row = left[k : k + 1, :], right[k : k + 1, :]
        root = 1.0 / jnp.sqrt(pivot)
        upper = jnp.where(row == k, left_row * root, upper)
        lower = jnp.where(row == k, right_row * root, lower)
        times = jnp.where(row > k, left[:, k : k + 1] / pivot, 0.0)
        left = left - times * left_row
        right = right - times * right_row
    coeff_ref[...] = jnp.where(col >= row, upper, 0.0) / jnp.sqrt(jnp.float32(length))
    linv_ref[...] = lower * jnp.sqrt(jnp.float32(length))


def factor(near, far, length):
    square = jax.ShapeDtypeStruct((near.shape[0],) * 2, jnp.float32)
    return pl.pallas_call(
        functools.partial(factor_kernel, length),
        out_shape=(square, square),
        in_specs=[pl.BlockSpec(memory_space=pltpu.VMEM)] * 2,
        out_specs=(pl.BlockSpec(memory_space=pltpu.VMEM),) * 2,
        compiler_params=pltpu.CompilerParams(vmem_limit_bytes=1 << 20),
        name="factor",
    )(near, far)


def basis_kernel(linv_ref, *refs):
    y_refs, out_ref, table = refs[:-2], refs[-2], refs[-1]
    cols, parts, _, nvar = out_ref.shape[:4]
    count = linv_ref.shape[0]
    af = lax.axis_index("af")
    for c in range(cols):
        line = linv_ref[pl.ds(af * cols + c, 1), :]
        for u in range(count):
            table[c * count + u] = jnp.broadcast_to(line[:, u : u + 1], (SUB, LANE))
    for k, y_ref in enumerate(y_refs):
        plane = lax.bitwise_xor(af, k)
        for part in range(parts):
            sums = [[None] * nvar for _ in range(cols)]
            for u in range(count):
                values = [y_ref[u, part * nvar + v] for v in range(nvar)]
                for c in range(cols):
                    times = table[c * count + u]
                    for v in range(nvar):
                        term = times * values[v]
                        sums[c][v] = term if u == 0 else sums[c][v] + term
            for c in range(cols):
                for v in range(nvar):
                    out_ref[c, part, plane, v, :, :LANE] = sums[c][v][: SUB // 2]
                    out_ref[c, part, plane, v, :, LANE:] = sums[c][v][SUB // 2 :]


def basis_of(linv, ys, shape):
    return pl.pallas_call(
        basis_kernel,
        out_shape=jax.ShapeDtypeStruct(shape, jnp.float32),
        in_specs=[pl.BlockSpec(memory_space=pltpu.VMEM)] * (1 + len(ys)),
        out_specs=pl.BlockSpec(memory_space=pltpu.VMEM),
        scratch_shapes=[pltpu.VMEM((shape[0] * linv.shape[0], SUB, LANE), jnp.float32)],
        compiler_params=pltpu.CompilerParams(vmem_limit_bytes=8 << 20),
        name="basis",
    )(linv, *ys)


def on_device(size_x, size_f, forcing, flow, sponge, coupling, omega):
    cols, parts, planes, nvar, rad, azi = forcing.shape
    groups = size_x // cols
    two_sided = groups != 2
    assert rad * azi == SUB * LANE and azi == 2 * LANE and size_x % cols == 0
    assert planes == size_f and 2 * planes == SWEEPS and cols == 4
    dims = (cols, parts, planes, nvar, groups)

    slabs = pack(forcing, sponge, flow)
    halo = []
    for k in range(cols):
        pairs = []
        for g in range(size_x):
            group, j = divmod(g, cols)
            target = group - 1 if j < cols // 2 else group + 1
            if 0 <= target < groups:
                pairs.append((g, target * cols + (j ^ k)))
        halo.append(lax.ppermute(slabs[k], "gx", pairs))
    mine = [slabs[0]]
    for k in range(1, cols):
        pairs = [(g, g ^ k) for g in range(size_x)]
        mine.append(lax.ppermute(slabs[k], "gx", pairs))
    state = sweeps(coupling, omega, mine, dims, two_sided)
    z = sweeps(coupling, omega, halo, dims, two_sided, state)[0]

    together = [
        [(q * cols + j) * size_f + a for a in range(size_f) for j in range(cols)] for q in range(groups)
    ]
    y = lax.all_to_all(z, ("gx", "af"), 0, 0, axis_index_groups=together, tiled=True)
    ys = [y] + [None] * (size_f - 1)
    ys[2] = lax.ppermute(y, "af", [(a, a ^ 2) for a in range(size_f)])
    ys[1] = lax.ppermute(y, "af", [(a, a ^ 1) for a in range(size_f)])
    g = add_up(lax.all_to_all(gram(y, size_x), "gx", 0, 0, tiled=True))
    g = g + lax.ppermute(g, "af", [(x, x ^ 1) for x in range(size_f)])
    far = lax.ppermute(g, "af", [(x, x ^ 2) for x in range(size_f)])
    far, ys[2] = lax.optimization_barrier((far, ys[2]))
    ys[3] = lax.ppermute(ys[2], "af", [(x, x ^ 1) for x in range(size_f)])
    length = parts * planes * nvar * rad * azi * size_x
    coeff, linv = factor(g, far, length)
    return basis_of(linv, ys, forcing.shape), coeff


def solution(mesh):
    placed = (
        P("af", None, "gx", None, None, None),
        P("gx", None, None),
        P("gx", None, None),
        P(),
        P(),
    )

    def body(*args):
        return on_device(mesh.shape["gx"], mesh.shape["af"], *args)

    return jax.shard_map(
        body,
        mesh=mesh,
        in_specs=placed,
        out_specs=(P("af", None, "gx", None, None, None), P()),
        check_vma=False,
    )
```
